128 devices in a mesh: row: 8 (over y_hi, x), col: 16 (over y_lo, z, core).
Axes of the slice: x: 4, y: 4 (y_hi: 2, y_lo: 2; y = y_hi * 2 + y_lo), z: 4, core: 2. Of those that a mesh axis runs over, the one named last changes fastest.
Arguments:
- samples: bfloat16 [1024, 200192], P(('row', 'col')), may hold values from -6 to 6
- pfb_taps: float32 [8, 512], replicated, may hold values from -2 to 2
- antenna_input_row: int32 [1024], replicated, may hold values from 0 to 1023, each once
- positions: float32 [2, 1024], P(None, ('row', 'col')), may hold values from -300 to 300
- directions: float32 [2, 1024], replicated, may hold values from -0.05 to 0.05
- pointing: int32 [1024], replicated, may hold values from 0 to 1023, each once
Outputs:
- visibilities: float32 [256, 2, 1024, 1024], P(('row', 'col'))
- beam_power: float32 [256, 24, 1024], P(('row', 'col'))
The draws below stay inside these ranges and needn't reach their ends.
Inputs may be any that keep to these rules, and one draw needn't show every extreme that they name: A permutation: antenna a's samples arrive in input row antenna_input_row[a]. A permutation: beam b points to table row pointing[b], each row used by exactly one beam.
All inputs are finite; a program needn't handle non-finite values.
Results may differ from the reference program's by a relative error of at most 0.0034.
Values may be sent and summed in bfloat16 or wider, within the bound.
A program may use at most 128 MiB of HBM per device.

```python
import math
import jax
import jax.numpy as jnp
from jax import lax

ANTENNA_COUNT = 1024
CHAN = 256
BEAMS = 1024
FILTER_TAPS = 8
NDIR = 1024
SPECTRA_PER_BLOCK = 128
BLOCKS = 3
INTEG = 16
FFT_LEN = 512
SPECTRUM_COUNT = 384
BINS = 24
SAMPLE_COUNT = 200192


def levels(key, extent, pieces, least, largest):
    def one(dim, blocks):
        draws = jax.random.uniform(jax.random.fold_in(jax.random.fold_in(key, 6), dim), (blocks,), jnp.float32, least / len(pieces), largest / len(pieces))
        return jnp.repeat(jnp.exp(draws), extent[dim] // blocks).reshape((-1,) + (1,) * (len(extent) - dim - 1))

    loudness = one(*pieces[0])
    for cut in pieces[1:]:
        loudness = loudness * one(*cut)
    return loudness


def centred(rng, shape, scale, bound, pieces=(), kind=jnp.bfloat16):
    level = levels(rng, shape, pieces, -0.22, 0.18) if pieces else 1.0
    values = jax.random.normal(rng, shape, jnp.float32) * scale * level
    return jnp.minimum(jnp.maximum(values, -bound), bound).astype(kind)


def setup_inputs(seed: int = 0) -> dict:
    seeds = jax.random.split(jax.random.key(seed), 7)
    return {
        "samples": centred(seeds[0], (ANTENNA_COUNT, SAMPLE_COUNT), 1.0, 6.0, ((0, 128),)),
        "pfb_taps": centred(seeds[1], (FILTER_TAPS, FFT_LEN), 0.35, 2.0, (), jnp.float32),
        "antenna_input_row": jax.random.permutation(seeds[2], ANTENNA_COUNT).astype(jnp.int32),
        "positions": jnp.clip(jax.random.uniform(seeds[3], (2, ANTENNA_COUNT), jnp.float32, -300.0, 300.0) * levels(seeds[3], (2, ANTENNA_COUNT), ((1, 128),), -0.4, 0.0), -300.0, 300.0),
        "directions": jnp.clip(jax.random.uniform(seeds[4], (2, NDIR), jnp.float32, -0.05, 0.05), -0.05, 0.05),
        "pointing": jax.random.permutation(seeds[5], BEAMS).astype(jnp.int32),
    }


def antenna_spectra(row, pfb_taps):
    item_count = BLOCKS * SPECTRA_PER_BLOCK
    framed_samples = row.astype(jnp.float32).reshape(item_count + FILTER_TAPS - 1, FFT_LEN)
    filtered_frames = jnp.zeros((item_count, FFT_LEN), jnp.float32)
    for tap in range(FILTER_TAPS):
        filtered_frames = filtered_frames + pfb_taps[tap][None, :] * framed_samples[tap:tap + item_count]
    spectrum_rows = jnp.fft.rfft(filtered_frames, axis=-1)[:, :CHAN]
    real_part = (jnp.real(spectrum_rows) / math.sqrt(FFT_LEN)).astype(jnp.float32)
    imag_part = (jnp.imag(spectrum_rows) / math.sqrt(FFT_LEN)).astype(jnp.float32)
    return jnp.stack([real_part, imag_part], 0).astype(jnp.bfloat16)

def reference(samples, pfb_taps, antenna_input_row, positions, directions, pointing):
    spectra = lax.map(lambda row: antenna_spectra(row, pfb_taps), samples)
    ordered = spectra[antenna_input_row]
    by_channel = jnp.transpose(ordered, (3, 0, 1, 2))
    chosen_dirs = jnp.take(directions, pointing, axis=1)
    cos_l = chosen_dirs[0]
    cos_m = chosen_dirs[1]
    delay = cos_l[:, None] * positions[0][None, :] + cos_m[:, None] * positions[1][None, :]
    scale_factor = 1.0 / math.sqrt(ANTENNA_COUNT)

    def per_channel(args):
        channel_spectra, channel = args
        plain_result = channel_spectra.reshape(ANTENNA_COUNT, 2 * SPECTRUM_COUNT)
        turned = jnp.concatenate([channel_spectra[:, 1], -channel_spectra[:, 0]], axis=1)
        stacked = jnp.concatenate([plain_result, turned], axis=0)
        gram_matrix = jnp.dot(stacked, plain_result.T, preferred_element_type=jnp.float32) / SPECTRUM_COUNT
        freq = (channel.astype(jnp.float32) + 1.0) * (2.0 * math.pi / CHAN)
        phase = freq * delay
        w_real = jnp.cos(phase) * scale_factor
        w_imag = -jnp.sin(phase) * scale_factor
        w_matrix = jnp.concatenate([jnp.concatenate([w_real, -w_imag], 1), jnp.concatenate([w_imag, w_real], 1)], 0).astype(jnp.bfloat16)
        column_list = jnp.transpose(channel_spectra, (1, 0, 2)).reshape(2 * ANTENNA_COUNT, SPECTRUM_COUNT)
        voltage = jnp.dot(w_matrix, column_list, preferred_element_type=jnp.float32)
        power = voltage[:BEAMS] * voltage[:BEAMS] + voltage[BEAMS:] * voltage[BEAMS:]
        binned_spectra = lax.optimization_barrier(jnp.sum(power.reshape(BEAMS, BINS, INTEG), axis=2))
        return (gram_matrix.reshape(2, ANTENNA_COUNT, ANTENNA_COUNT), binned_spectra.T)
    channels = jnp.arange(CHAN, dtype=jnp.int32)
    visibilities, beam_power = lax.map(per_channel, (by_channel, channels))
    return (visibilities, beam_power)
```

```python
import functools
import math

import jax
import jax.numpy as jnp
import ml_dtypes
import numpy as np
from jax import lax
from jax.experimental import pallas as pl
from jax.experimental.pallas import tpu as pltpu
from jax.sharding import PartitionSpec as P

MESH = pl.DeviceIdType.MESH
ROWS, COLS = 8, 16
DEVICES = ROWS * COLS
ANT = 1024
BEAMS = 1024
LOCAL = 8
FRAME = 512
HALF = 256
TAPS = 8
CHUNKS = 3
SPC = 128
SPECTRA = CHUNKS * SPC
INTEG = 16
CHANNELS = 256
NT = (((1,), (1,)), ((), ()))
NN = (((1,), (0,)), ((), ()))
F32, BF16 = jnp.float32, jnp.bfloat16


def dft_tables():
    n = np.arange(HALF)
    d = np.arange(CHANNELS // 2)
    tables = []
    for parity in range(2):
        angle = 2.0 * np.pi * ((2 * d[:, None] + parity) * n[None, :] % FRAME) / FRAME
        tables.append(np.concatenate([np.cos(angle), -np.sin(angle)], 0) / math.sqrt(FRAME))
    table = np.stack(tables)
    high = table.astype(ml_dtypes.bfloat16)
    low = (table - high.astype(np.float64)).astype(ml_dtypes.bfloat16)
    return high, low


def sine_coefficients():
    theta = (np.arange(4000) + 0.5) * np.pi / 8000
    w = 0.25 * np.cos(theta)
    basis = np.stack([w ** (2 * j + 1) for j in range(6)], 1)
    return np.linalg.lstsq(basis, np.sin(2 * np.pi * w), rcond=None)[0]


SINE = [float(v) / math.sqrt(ANT) for v in sine_coefficients()]


def sine(w):
    z = w * w
    acc = SINE[-1] * z + SINE[-2]
    for coefficient in SINE[-3::-1]:
        acc = acc * z + coefficient
    return acc * w


def column(row):
    return jnp.transpose(jnp.broadcast_to(row.astype(F32), (128, 128)))


def main_kernel(samples, taps, thigh, tlow, antrow, pos, dirs, pointing,
                xs, beam,
                eo, stage, send, recv, pos1, pos2, table, weights, perm, lcol, mcol, plain, full,
                lsem, ssem, rsem, psem, qsem):
    r, c = lax.axis_index("row"), lax.axis_index("col")
    me = r * COLS + c
    cts = [lax.rem(c + k, COLS) for k in range(COLS)]

    def each(fn):
        def outer(j, carry):
            for k in range(COLS):
                rt = lax.rem(r + j + (3 * k) % ROWS, ROWS)
                if k == 0:
                    @pl.when(j > 0)
                    def _():
                        fn(rt, cts[0])
                else:
                    fn(rt, cts[k])
            return carry
        lax.fori_loop(0, ROWS, outer, 0)

    barrier = pltpu.get_barrier_semaphore()
    each(lambda rt, ct: pl.semaphore_signal(barrier, inc=1, device_id=(rt, ct), device_id_type=MESH))

    def channelize(chunk):
        def filt(u, carry):
            first = chunk * SPC + 8 * u
            for j in range(2):
                halves = []
                for lane in (j * 128, j * 128 + HALF):
                    frames = [
                        samples[:, pl.ds(pl.multiple_of((first + f) * FRAME + lane, 128), 128)].astype(F32)
                        for f in range(8 + TAPS - 1)
                    ]
                    tap = [jnp.broadcast_to(taps[t:t + 1, lane:lane + 128], (8, 128)) for t in range(TAPS)]
                    sums = []
                    for s in range(8):
                        acc = tap[0] * frames[s]
                        for t in range(1, TAPS):
                            acc = acc + tap[t] * frames[s + t]
                        sums.append(acc)
                    halves.append(sums)
                for s in range(8):
                    at = pl.ds(8 * u + s, 8, stride=SPC)
                    eo[j, at, :] = halves[0][s] + halves[1][s]
                    eo[2 + j, at, :] = halves[0][s] - halves[1][s]
            return carry
        lax.fori_loop(0, SPC // 8, filt, 0)

        def dft(g, carry):
            for p in range(2):
                rows = pl.ds(pl.multiple_of(g * 256, 256), 256)
                x = jnp.concatenate([eo[2 * p, rows, :], eo[2 * p + 1, rows, :]], 1)
                hi = x.astype(BF16)
                lo = (x - hi.astype(F32)).astype(BF16)
                res = lax.dot_general(thigh[p], hi, NT, preferred_element_type=F32)
                res = res + lax.dot_general(thigh[p], lo, NT, preferred_element_type=F32)
                res = res + lax.dot_general(tlow[p], hi, NT, preferred_element_type=F32)
                for q in range(2):
                    for i in range(2):
                        stage[pl.ds(p * 16 + q * 8 + i + 2 * g, 128, stride=32), :] = (
                            res[q * 128:(q + 1) * 128, i * 128:(i + 1) * 128])
            return carry
        lax.fori_loop(0, LOCAL // 2, dft, 0)

        def pack(u, carry):
            block = stage[pl.ds(pl.multiple_of(u * 256, 256), 256), :]
            send[chunk, pl.ds(u * 8, 8)] = block.reshape(8, 32, 128).astype(BF16)
            return carry
        lax.fori_loop(0, 16, pack, 0)

    def launch(chunk):
        each(lambda rt, ct: pltpu.make_async_remote_copy(
            src_ref=send.at[chunk, rt * COLS + ct], dst_ref=recv.at[chunk, me],
            send_sem=ssem.at[chunk], recv_sem=rsem.at[chunk],
            device_id=(rt, ct), device_id_type=MESH).start())
        pltpu.make_async_copy(send.at[chunk, me], recv.at[chunk, me], lsem.at[chunk]).start()

    channelize(0)
    pl.semaphore_wait(barrier, DEVICES - 1)
    launch(0)
    pltpu.make_async_copy(pos, pos1.at[r], lsem.at[3]).start()
    for j in range(1, ROWS):
        pltpu.make_async_remote_copy(
            src_ref=pos, dst_ref=pos1.at[r], send_sem=psem.at[0], recv_sem=psem.at[1],
            device_id=(lax.rem(r + j, ROWS), c), device_id_type=MESH).start()
    channelize(1)
    launch(1)
    pltpu.make_async_copy(pos, pos1.at[r], lsem.at[3]).wait()
    pltpu.make_async_copy(pos1.at[pl.ds(0, ROWS - 1)], pos1.at[pl.ds(0, ROWS - 1)], psem.at[0]).wait()
    pltpu.make_async_copy(pos1.at[pl.ds(0, ROWS - 1)], pos1.at[pl.ds(0, ROWS - 1)], psem.at[1]).wait()
    pltpu.make_async_copy(pos1, pos2.at[c], lsem.at[3]).start()
    for k in range(1, COLS):
        pltpu.make_async_remote_copy(
            src_ref=pos1, dst_ref=pos2.at[c], send_sem=qsem.at[0], recv_sem=qsem.at[1],
            device_id=(r, cts[k]), device_id_type=MESH).start()
    channelize(2)
    launch(2)

    lane = lax.broadcasted_iota(jnp.int32, (128, 128), 1).astype(F32)
    for blk in range(8):
        wanted = column(antrow[blk:blk + 1, :])
        for t in range(8):
            perm[blk * 128:(blk + 1) * 128, t * 128:(t + 1) * 128] = (
                jnp.where(wanted == lane + 128.0 * t, 1.0, 0.0).astype(BF16))
        wanted = column(pointing[blk:blk + 1, :])
        l_sum = jnp.zeros((128, 128), F32)
        m_sum = jnp.zeros((128, 128), F32)
        for t in range(8):
            hit = wanted == lane + 128.0 * t
            l_sum = l_sum + jnp.where(hit, dirs[0:1, t * 128:(t + 1) * 128], 0.0)
            m_sum = m_sum + jnp.where(hit, dirs[1:2, t * 128:(t + 1) * 128], 0.0)
        lcol[blk * 128:(blk + 1) * 128, :] = jnp.broadcast_to(jnp.sum(l_sum, 1, keepdims=True), (128, 128))
        mcol[blk * 128:(blk + 1) * 128, :] = jnp.broadcast_to(jnp.sum(m_sum, 1, keepdims=True), (128, 128))

    pltpu.make_async_copy(pos1, pos2.at[c], lsem.at[3]).wait()
    for s in range(2):
        pltpu.make_async_copy(pos2.at[pl.ds(0, COLS - 1)], pos2.at[pl.ds(0, COLS - 1)], qsem.at[s]).wait()

    def spread(i, carry):
        table[pl.ds(i, 1), :] = pos2[i // ROWS, i % ROWS]
        return carry
    lax.fori_loop(0, DEVICES, spread, 0)
    rest = table[...]
    parts = []
    for _ in range(3):
        part = rest.astype(BF16)
        rest = rest - part.astype(F32)
        parts.append(part)
    picked = []
    antenna = lax.broadcasted_iota(jnp.int32, (128, ANT), 1)
    entry = lax.broadcasted_iota(jnp.int32, (128, ANT), 0)
    mine = (entry % ROWS) * COLS + entry // ROWS == antenna // LOCAL
    for xy in range(2):
        pick = jnp.where(entry == antenna % LOCAL + LOCAL * xy, 1.0, 0.0).astype(BF16)
        whole = sum(lax.dot_general(part, pick, NN, preferred_element_type=F32) for part in parts[::-1])
        picked.append(jnp.sum(jnp.where(mine, whole, 0.0), 0, keepdims=True))
    xpos, ypos = picked

    factors = [(2 * me + p + 1).astype(F32) * (1.0 / CHANNELS) for p in range(2)]

    def weigh(u, carry):
        rows = pl.ds(pl.multiple_of(u * 16, 16), 16)
        l_here, m_here = lcol[rows, :], mcol[rows, :]
        for t in range(8):
            cols = slice(t * 128, (t + 1) * 128)
            delay = l_here * xpos[:, cols] + m_here * ypos[:, cols]
            for p in range(2):
                turns = delay * factors[p]
                turns = turns - jnp.round(turns)
                weights[p, rows, t * 128:(t + 1) * 128] = sine(0.25 - jnp.abs(turns)).astype(BF16)
                w = 0.25 - jnp.abs(0.25 - turns)
                weights[p, rows, ANT + t * 128:ANT + (t + 1) * 128] = sine(jnp.maximum(w, -0.5 - w)).astype(BF16)
        return carry
    lax.fori_loop(0, BEAMS // 16, weigh, 0)

    for chunk in range(CHUNKS):
        pltpu.make_async_copy(send.at[chunk, me], recv.at[chunk, me], lsem.at[chunk]).wait()
        every = pl.ds(0, DEVICES - 1)
        pltpu.make_async_copy(send.at[chunk, every], recv.at[chunk, every], rsem.at[chunk]).wait()
        for p in range(2):
            def gather(u, carry):
                z = recv[chunk, pl.ds(u * 16, 16), p * 16:(p + 1) * 16, :].astype(F32)
                rows = pl.ds(pl.multiple_of(u * 128, 128), 128)
                plain[rows, 0:128] = z[:, 0:8, :].reshape(128, 128).astype(BF16)
                plain[rows, 128:256] = z[:, 8:16, :].reshape(128, 128).astype(BF16)
                return carry
            lax.fori_loop(0, 8, gather, 0)

            def order(u, carry):
                rows = pl.ds(pl.multiple_of(u * 256, 256), 256)
                x = lax.dot_general(perm[rows, :], plain[...], NN, preferred_element_type=F32)
                xb = x.astype(BF16)
                full[rows, :] = xb
                xs[p, rows, chunk * 256:(chunk + 1) * 256] = xb
                below = pl.ds(pl.multiple_of(ANT + u * 256, 256), 256)
                full[below, 0:128] = x[:, 128:256].astype(BF16)
                full[below, 128:256] = (-x[:, 0:128]).astype(BF16)
                return carry
            lax.fori_loop(0, 4, order, 0)

            def form(u, carry):
                rows = pl.ds(pl.multiple_of(u * 256, 256), 256)
                v = lax.dot_general(weights[p, rows, :], full[...], NN, preferred_element_type=F32)
                power = v[:, 0:128] * v[:, 0:128] + v[:, 128:256] * v[:, 128:256]
                bins = jnp.sum(jnp.transpose(power).reshape(SPC // INTEG, INTEG, 256), axis=1)
                beam[p, chunk * 8:(chunk + 1) * 8, pl.ds(pl.multiple_of(u * 256, 256), 256)] = bins
                return carry
            lax.fori_loop(0, 4, form, 0)

    for chunk in range(CHUNKS):
        every = pl.ds(0, DEVICES - 1)
        pltpu.make_async_copy(send.at[chunk, every], recv.at[chunk, every], ssem.at[chunk]).wait()


def gram_kernel(x, out):
    u = pl.program_id(1)
    left = x[0, pl.ds(pl.multiple_of(u * 256, 256), 256), :]
    scale = 1.0 / SPECTRA
    out[0, 0] = lax.dot_general(left, x[0], NT, preferred_element_type=F32) * scale
    turned = jnp.concatenate(
        [piece for k in range(CHUNKS) for piece in (left[:, k * 256 + 128:(k + 1) * 256], -left[:, k * 256:k * 256 + 128])], 1)
    out[0, 1] = lax.dot_general(turned, x[0], NT, preferred_element_type=F32) * scale


def body(samples, pfb_taps, antenna_input_row, positions, directions, pointing):
    high, low = dft_tables()
    pos = jnp.pad(positions.reshape(1, 2 * LOCAL), ((0, 0), (0, 128 - 2 * LOCAL)))
    vmem = pl.BlockSpec(memory_space=pltpu.VMEM)
    xs, beam = pl.pallas_call(
        main_kernel,
        out_shape=(jax.ShapeDtypeStruct((2, ANT, 2 * SPECTRA), BF16),
                   jax.ShapeDtypeStruct((2, SPECTRA // INTEG, BEAMS), F32)),
        in_specs=[vmem] * 8,
        out_specs=(vmem, vmem),
        scratch_shapes=[
            pltpu.VMEM((4, LOCAL * SPC, 128), F32),
            pltpu.VMEM((DEVICES * 32, 128), F32),
            pltpu.VMEM((CHUNKS, DEVICES, 32, 128), BF16),
            pltpu.VMEM((CHUNKS, DEVICES, 32, 128), BF16),
            pltpu.VMEM((ROWS, 1, 128), F32),
            pltpu.VMEM((COLS, ROWS, 1, 128), F32),
            pltpu.VMEM((DEVICES, 128), F32),
            pltpu.VMEM((2, BEAMS, 2 * ANT), BF16),
            pltpu.VMEM((ANT, ANT), BF16),
            pltpu.VMEM((BEAMS, 128), F32),
            pltpu.VMEM((BEAMS, 128), F32),
            pltpu.VMEM((ANT, 256), BF16),
            pltpu.VMEM((2 * ANT, 256), BF16),
            pltpu.SemaphoreType.DMA((4,)),
            pltpu.SemaphoreType.DMA((CHUNKS,)),
            pltpu.SemaphoreType.DMA((CHUNKS,)),
            pltpu.SemaphoreType.DMA((2,)),
            pltpu.SemaphoreType.DMA((2,)),
        ],
        compiler_params=pltpu.CompilerParams(
            collective_id=0, has_side_effects=True, vmem_limit_bytes=60 * 1024 * 1024),
        name="channelize_exchange_beams",
    )(samples, pfb_taps, jnp.asarray(high), jnp.asarray(low), antenna_input_row.reshape(8, 128), pos,
      directions, pointing.reshape(8, 128))
    vis = pl.pallas_call(
        gram_kernel,
        grid=(2, 4),
        out_shape=jax.ShapeDtypeStruct((2, 2, ANT, ANT), F32),
        in_specs=[pl.BlockSpec((1, ANT, 2 * SPECTRA), lambda p, u: (p, 0, 0))],
        out_specs=pl.BlockSpec((1, 2, 256, ANT), lambda p, u: (p, 0, u, 0)),
        compiler_params=pltpu.CompilerParams(vmem_limit_bytes=40 * 1024 * 1024),
        name="visibilities",
    )(xs)
    return vis, beam


def solution(mesh):
    return jax.shard_map(
        body,
        mesh=mesh,
        in_specs=(P(("row", "col"), None), P(), P(), P(None, ("row", "col")), P(), P()),
        out_specs=(P(("row", "col"), None, None, None), P(("row", "col"), None, None)),
        check_vma=False,
    )
```

```python
import functools
import math

import jax
import jax.numpy as jnp
import ml_dtypes
import numpy as np
from jax import lax
from jax.experimental import pallas as pl
from jax.experimental.pallas import tpu as pltpu
from jax.sharding import PartitionSpec as P

MESH = pl.DeviceIdType.MESH
ROWS, COLS = 8, 16
DEVICES = ROWS * COLS
ANT = 1024
BEAMS = 1024
LOCAL = 8
FRAME = 512
HALF = 256
TAPS = 8
CHUNKS = 3
SPC = 128
SPECTRA = CHUNKS * SPC
INTEG = 16
PITCH = SPC + 1
BLOCK = 33
CHANNELS = 256
NT = (((1,), (1,)), ((), ()))
NN = (((1,), (0,)), ((), ()))
F32, BF16 = jnp.float32, jnp.bfloat16


def dft_tables():
    n = np.arange(HALF)
    d = np.arange(CHANNELS // 2)
    tables = []
    for parity in range(2):
        angle = 2.0 * np.pi * ((2 * d[:, None] + parity) * n[None, :] % FRAME) / FRAME
        tables.append(np.concatenate([np.cos(angle), -np.sin(angle)], 0) / math.sqrt(FRAME))
    table = np.stack(tables)
    high = table.astype(ml_dtypes.bfloat16)
    low = (table - high.astype(np.float64)).astype(ml_dtypes.bfloat16)
    return high, low


def sine_coefficients():
    theta = (np.arange(4000) + 0.5) * np.pi / 8000
    w = 0.25 * np.cos(theta)
    basis = np.stack([w ** (2 * j + 1) for j in range(5)], 1)
    return np.linalg.lstsq(basis, np.sin(2 * np.pi * w), rcond=None)[0]


SINE = [float(v) / math.sqrt(ANT) for v in sine_coefficients()]


def sine(w):
    z = w * w
    acc = SINE[-1] * z + SINE[-2]
    for coefficient in SINE[-3::-1]:
        acc = acc * z + coefficient
    return acc * w


def column(row):
    return jnp.transpose(jnp.broadcast_to(row.astype(F32), (128, 128)))


def main_kernel(samples, taps, thigh, tlow, antrow, pos, dirs, pointing,
                xs, beam,
                eo, stage, send, recv, pos1, pos2, table, weights, perm, lcol, mcol, plain, full,
                lsem, ssem, rsem, psem, qsem):
    r, c = lax.axis_index("row"), lax.axis_index("col")
    me = r * COLS + c

    def peer(i):
        k, j = lax.rem(i, COLS), lax.div(i, COLS)
        return lax.rem(r + j + 3 * k, ROWS), lax.rem(c + k, COLS)

    barrier = pltpu.get_barrier_semaphore()

    def greet(first, count):
        for v in range(count):
            pl.semaphore_signal(barrier, inc=1, device_id=peer(first + v), device_id_type=MESH)

    def launch(chunk, first, count):
        for v in range(count):
            rt, ct = peer(first + v)
            pltpu.make_async_remote_copy(
                src_ref=send.at[chunk, rt * COLS + ct], dst_ref=recv.at[chunk, me],
                send_sem=ssem.at[chunk], recv_sem=rsem.at[chunk],
                device_id=(rt, ct), device_id_type=MESH).start()

    def own(chunk):
        return pltpu.make_async_copy(send.at[chunk, me], recv.at[chunk, me], lsem.at[chunk])

    def channelize(chunk):
        def filt(u, carry):
            first = chunk * SPC + 8 * u
            for j in range(2):
                halves = []
                for lane in (j * 128, j * 128 + HALF):
                    frames = [
                        samples[:, pl.ds(pl.multiple_of((first + f) * FRAME + lane, 128), 128)].astype(F32)
                        for f in range(8 + TAPS - 1)
                    ]
                    tap = [jnp.broadcast_to(taps[t:t + 1, lane:lane + 128], (8, 128)) for t in range(TAPS)]
                    sums = []
                    for s in range(8):
                        acc = tap[0] * frames[s]
                        for t in range(1, TAPS):
                            acc = acc + tap[t] * frames[s + t]
                        sums.append(acc)
                    halves.append(sums)
                for s in range(8):
                    at = pl.ds(8 * u + s, 8, stride=PITCH)
                    eo[j, at, :] = halves[0][s] + halves[1][s]
                    eo[2 + j, at, :] = halves[0][s] - halves[1][s]
            if chunk > 0:
                launch(chunk - 1, 1 + 5 * u, 5)
            return carry

        if chunk == 0:
            def greeting(u, carry):
                greet(1 + 8 * u, 8)
                return filt(u, carry)
            lax.fori_loop(0, SPC // 8 - 1, greeting, 0)
            greet(DEVICES - 7, 7)
            filt(SPC // 8 - 1, 0)
        else:
            lax.fori_loop(0, SPC // 8, filt, 0)

        def dft(g, carry):
            for p in range(2):
                x = jnp.concatenate([
                    jnp.concatenate([eo[2 * p + j, pl.ds((2 * g + i) * PITCH, SPC), :] for j in range(2)], 1)
                    for i in range(2)], 0)
                hi = x.astype(BF16)
                lo = (x - hi.astype(F32)).astype(BF16)
                res = lax.dot_general(thigh[p], hi, NT, preferred_element_type=F32)
                res = res + lax.dot_general(thigh[p], lo, NT, preferred_element_type=F32)
                res = res + lax.dot_general(tlow[p], hi, NT, preferred_element_type=F32)
                for q in range(2):
                    for i in range(2):
                        stage[pl.ds(p * 16 + q * 8 + i + 2 * g, 128, stride=BLOCK), :] = (
                            res[q * 128:(q + 1) * 128, i * 128:(i + 1) * 128])
            if chunk > 0:
                launch(chunk - 1, 81 + 8 * g, 8)
            return carry
        lax.fori_loop(0, LOCAL // 2, dft, 0)

        def pack(u, carry):
            for d in range(8):
                block = stage[pl.ds((u * 8 + d) * BLOCK, 32), :]
                send[chunk, u * 8 + d] = block.astype(BF16)
            return carry

        def packing(u, carry):
            if chunk > 0:
                launch(chunk - 1, 113 + u, 1)
            return pack(u, carry)
        lax.fori_loop(0, 15, packing, 0)
        pack(15, 0)
        if chunk > 0:
            own(chunk - 1).start()

    channelize(0)
    pl.semaphore_wait(barrier, DEVICES - 1)
    pltpu.make_async_copy(pos, pos1.at[r], lsem.at[3]).start()
    for j in range(1, ROWS):
        pltpu.make_async_remote_copy(
            src_ref=pos, dst_ref=pos1.at[r], send_sem=psem.at[0], recv_sem=psem.at[1],
            device_id=(lax.rem(r + j, ROWS), c), device_id_type=MESH).start()
    channelize(1)
    pltpu.make_async_copy(pos, pos1.at[r], lsem.at[3]).wait()
    pltpu.make_async_copy(pos1.at[pl.ds(0, ROWS - 1)], pos1.at[pl.ds(0, ROWS - 1)], psem.at[0]).wait()
    pltpu.make_async_copy(pos1.at[pl.ds(0, ROWS - 1)], pos1.at[pl.ds(0, ROWS - 1)], psem.at[1]).wait()
    pltpu.make_async_copy(pos1, pos2.at[c], lsem.at[3]).start()
    for k in range(1, COLS):
        pltpu.make_async_remote_copy(
            src_ref=pos1, dst_ref=pos2.at[c], send_sem=qsem.at[0], recv_sem=qsem.at[1],
            device_id=(r, lax.rem(c + k, COLS)), device_id_type=MESH).start()
    channelize(2)
    own(2).start()

    lane = lax.broadcasted_iota(jnp.int32, (128, 128), 1).astype(F32)
    for blk in range(8):
        wanted = column(antrow[blk:blk + 1, :])
        for t in range(8):
            perm[blk * 128:(blk + 1) * 128, t * 128:(t + 1) * 128] = (
                jnp.where(wanted == lane + 128.0 * t, 1.0, 0.0).astype(BF16))
        wanted = column(pointing[blk:blk + 1, :])
        l_sum = jnp.zeros((128, 128), F32)
        m_sum = jnp.zeros((128, 128), F32)
        for t in range(8):
            hit = wanted == lane + 128.0 * t
            l_sum = l_sum + jnp.where(hit, dirs[0:1, t * 128:(t + 1) * 128], 0.0)
            m_sum = m_sum + jnp.where(hit, dirs[1:2, t * 128:(t + 1) * 128], 0.0)
        lcol[blk * 128:(blk + 1) * 128, :] = jnp.broadcast_to(jnp.sum(l_sum, 1, keepdims=True), (128, 128))
        mcol[blk * 128:(blk + 1) * 128, :] = jnp.broadcast_to(jnp.sum(m_sum, 1, keepdims=True), (128, 128))

    pltpu.make_async_copy(pos1, pos2.at[c], lsem.at[3]).wait()
    for s in range(2):
        pltpu.make_async_copy(pos2.at[pl.ds(0, COLS - 1)], pos2.at[pl.ds(0, COLS - 1)], qsem.at[s]).wait()

    def spread(i, carry):
        table[pl.ds(i, 1), :] = pos2[i // ROWS, i % ROWS]
        return carry
    lax.fori_loop(0, DEVICES, spread, 0)
    rest = table[...]
    parts = []
    for _ in range(3):
        part = rest.astype(BF16)
        rest = rest - part.astype(F32)
        parts.append(part)
    picked = []
    antenna = lax.broadcasted_iota(jnp.int32, (128, ANT), 1)
    entry = lax.broadcasted_iota(jnp.int32, (128, ANT), 0)
    mine = (entry % ROWS) * COLS + entry // ROWS == antenna // LOCAL
    for xy in range(2):
        pick = jnp.where(entry == antenna % LOCAL + LOCAL * xy, 1.0, 0.0).astype(BF16)
        whole = sum(lax.dot_general(part, pick, NN, preferred_element_type=F32) for part in parts[::-1])
        picked.append(jnp.sum(jnp.where(mine, whole, 0.0), 0, keepdims=True))
    xpos, ypos = picked

    factors = [(2 * me + p + 1).astype(F32) * (1.0 / CHANNELS) for p in range(2)]

    def weigh(u, carry):
        rows = pl.ds(pl.multiple_of(u * 16, 16), 16)
        l_here, m_here = lcol[rows, :], mcol[rows, :]
        for t in range(8):
            cols = slice(t * 128, (t + 1) * 128)
            delay = l_here * xpos[:, cols] + m_here * ypos[:, cols]
            for p in range(2):
                turns = delay * factors[p]
                turns = turns - jnp.round(turns)
                weights[p, rows, t * 128:(t + 1) * 128] = sine(0.25 - jnp.abs(turns)).astype(BF16)
                w = 0.25 - jnp.abs(0.25 - turns)
                weights[p, rows, ANT + t * 128:ANT + (t + 1) * 128] = sine(jnp.maximum(w, -0.5 - w)).astype(BF16)
        return carry

    def weighing(u, carry):
        launch(CHUNKS - 1, 1 + 2 * u, 2)
        return weigh(u, carry)
    lax.fori_loop(0, BEAMS // 16 - 1, weighing, 0)
    launch(CHUNKS - 1, DEVICES - 1, 1)
    weigh(BEAMS // 16 - 1, 0)

    def beams(chunk, carry):
        own(chunk).wait()
        every = pl.ds(0, DEVICES - 1)
        pltpu.make_async_copy(send.at[chunk, every], recv.at[chunk, every], rsem.at[chunk]).wait()
        lanes = pl.ds(pl.multiple_of(chunk * 256, 256), 256)

        def channel(p, carry):
            def gather(u, carry):
                z = recv[chunk, pl.ds(u * 16, 16), pl.ds(pl.multiple_of(p * 16, 16), 16), :].astype(F32)
                rows = pl.ds(pl.multiple_of(u * 128, 128), 128)
                plain[rows, 0:128] = z[:, 0:8, :].reshape(128, 128).astype(BF16)
                plain[rows, 128:256] = z[:, 8:16, :].reshape(128, 128).astype(BF16)
                return carry
            lax.fori_loop(0, 8, gather, 0)
            x = lax.dot_general(perm[...], plain[...], NN, preferred_element_type=F32)
            xb = x.astype(BF16)
            full[0:ANT, :] = xb
            xs[p, :, lanes] = xb
            full[ANT:2 * ANT, 0:128] = x[:, 128:256].astype(BF16)
            full[ANT:2 * ANT, 128:256] = (-x[:, 0:128]).astype(BF16)
            v = lax.dot_general(weights[p], full[...], NN, preferred_element_type=F32)
            power = v[:, 0:128] * v[:, 0:128] + v[:, 128:256] * v[:, 128:256]
            bins = jnp.sum(jnp.transpose(power).reshape(SPC // INTEG, INTEG, BEAMS), axis=1)
            beam[p, pl.ds(pl.multiple_of(chunk * 8, 8), 8), :] = bins
            return carry
        return lax.fori_loop(0, 2, channel, carry)
    lax.fori_loop(0, CHUNKS, beams, 0)

    for chunk in range(CHUNKS):
        every = pl.ds(0, DEVICES - 1)
        pltpu.make_async_copy(send.at[chunk, every], recv.at[chunk, every], ssem.at[chunk]).wait()


def gram_kernel(x, out):
    u = pl.program_id(1)
    right = x[0, pl.ds(pl.multiple_of(u * 256, 256), 256), :]
    scale = 1.0 / SPECTRA
    out[0, 0] = lax.dot_general(x[0], right, NT, preferred_element_type=F32) * scale
    turned = jnp.concatenate(
        [piece for k in range(CHUNKS) for piece in (-right[:, k * 256 + 128:(k + 1) * 256], right[:, k * 256:k * 256 + 128])], 1)
    out[0, 1] = lax.dot_general(x[0], turned, NT, preferred_element_type=F32) * scale


def body(samples, pfb_taps, antenna_input_row, positions, directions, pointing):
    high, low = dft_tables()
    pos = jnp.pad(positions.reshape(1, 2 * LOCAL), ((0, 0), (0, 128 - 2 * LOCAL)))
    vmem = pl.BlockSpec(memory_space=pltpu.VMEM)
    xs, beam = pl.pallas_call(
        main_kernel,
        out_shape=(jax.ShapeDtypeStruct((2, ANT, 2 * SPECTRA), BF16),
                   jax.ShapeDtypeStruct((2, SPECTRA // INTEG, BEAMS), F32)),
        in_specs=[vmem] * 8,
        out_specs=(vmem, vmem),
        scratch_shapes=[
            pltpu.VMEM((4, LOCAL * PITCH, 128), F32),
            pltpu.VMEM((DEVICES * BLOCK, 128), F32),
            pltpu.VMEM((CHUNKS, DEVICES, 32, 128), BF16),
            pltpu.VMEM((CHUNKS, DEVICES, 32, 128), BF16),
            pltpu.VMEM((ROWS, 1, 128), F32),
            pltpu.VMEM((COLS, ROWS, 1, 128), F32),
            pltpu.VMEM((DEVICES, 128), F32),
            pltpu.VMEM((2, BEAMS, 2 * ANT), BF16),
            pltpu.VMEM((ANT, ANT), BF16),
            pltpu.VMEM((BEAMS, 128), F32),
            pltpu.VMEM((BEAMS, 128), F32),
            pltpu.VMEM((ANT, 256), BF16),
            pltpu.VMEM((2 * ANT, 256), BF16),
            pltpu.SemaphoreType.DMA((4,)),
            pltpu.SemaphoreType.DMA((CHUNKS,)),
            pltpu.SemaphoreType.DMA((CHUNKS,)),
            pltpu.SemaphoreType.DMA((2,)),
            pltpu.SemaphoreType.DMA((2,)),
        ],
        compiler_params=pltpu.CompilerParams(
            collective_id=0, has_side_effects=True, vmem_limit_bytes=60 * 1024 * 1024),
        name="channelize_exchange_beams",
    )(samples, pfb_taps, jnp.asarray(high), jnp.asarray(low), antenna_input_row.reshape(8, 128), pos,
      directions, pointing.reshape(8, 128))
    vis = pl.pallas_call(
        gram_kernel,
        grid=(2, 4),
        out_shape=jax.ShapeDtypeStruct((2, 2, ANT, ANT), F32),
        in_specs=[pl.BlockSpec((1, ANT, 2 * SPECTRA), lambda p, u: (p, 0, 0))],
        out_specs=pl.BlockSpec((1, 2, ANT, 256), lambda p, u: (p, 0, 0, u)),
        compiler_params=pltpu.CompilerParams(vmem_limit_bytes=40 * 1024 * 1024),
        name="visibilities",
    )(xs)
    return vis, beam


def solution(mesh):
    return jax.shard_map(
        body,
        mesh=mesh,
        in_specs=(P(("row", "col"), None), P(), P(), P(None, ("row", "col")), P(), P()),
        out_specs=(P(("row", "col"), None, None, None), P(("row", "col"), None, None)),
        check_vma=False,
    )
```

```python
import functools
import math

import jax
import jax.numpy as jnp
import ml_dtypes
import numpy as np
from jax import lax
from jax.experimental import pallas as pl
from jax.experimental.pallas import tpu as pltpu
from jax.sharding import PartitionSpec as P

MESH = pl.DeviceIdType.MESH
ROWS, COLS = 8, 16
DEVICES = ROWS * COLS
ANT = 1024
BEAMS = 1024
LOCAL = 8
FRAME = 512
HALF = 256
TAPS = 8
CHUNKS = 3
SPC = 128
SPECTRA = CHUNKS * SPC
INTEG = 16
PITCH = SPC + 1
BLOCK = 33
CHANNELS = 256
NT = (((1,), (1,)), ((), ()))
NN = (((1,), (0,)), ((), ()))
F32, BF16 = jnp.float32, jnp.bfloat16


def dft_tables():
    n = np.arange(HALF)
    d = np.arange(CHANNELS // 2)
    tables = []
    for parity in range(2):
        angle = 2.0 * np.pi * ((2 * d[:, None] + parity) * n[None, :] % FRAME) / FRAME
        tables.append(np.concatenate([np.cos(angle), -np.sin(angle)], 0) / math.sqrt(FRAME))
    table = np.stack(tables)
    high = table.astype(ml_dtypes.bfloat16)
    low = (table - high.astype(np.float64)).astype(ml_dtypes.bfloat16)
    return high, low


def sine_coefficients():
    theta = (np.arange(4000) + 0.5) * np.pi / 8000
    w = 0.25 * np.cos(theta)
    basis = np.stack([w ** (2 * j + 1) for j in range(5)], 1)
    return np.linalg.lstsq(basis, np.sin(2 * np.pi * w), rcond=None)[0]


SINE = [float(v) / math.sqrt(ANT) for v in sine_coefficients()]


def sine(w):
    z = w * w
    acc = SINE[-1] * z + SINE[-2]
    for coefficient in SINE[-3::-1]:
        acc = acc * z + coefficient
    return acc * w


def column(row):
    return jnp.transpose(jnp.broadcast_to(row.astype(F32), (128, 128)))


def main_kernel(samples_hbm, taps_hbm, thigh_hbm, tlow_hbm, antrow_hbm, place_hbm, dirs_hbm, pointing_hbm,
                xs, beam,
                eo, stage, send, recv, pos1, pos2, table, weights, perm, lcol, mcol, full, pos,
                samples, taps, thigh, tlow, antrow, place, dirs, pointing,
                lsem, ssem, rsem, psem, qsem, isem):
    needed = [0] + [(k * SPC + TAPS - 1) * FRAME for k in range(1, CHUNKS + 1)]
    slabs = [pltpu.make_async_copy(
        samples_hbm.at[:, lo:hi], samples.at[:, lo:hi], isem.at[7 + k])
        for k, (lo, hi) in enumerate(zip(needed[:-1], needed[1:]))]
    small = [pltpu.make_async_copy(src, dst, isem.at[k]) for k, (src, dst) in enumerate((
        (place_hbm, place), (taps_hbm, taps), (thigh_hbm, thigh), (tlow_hbm, tlow),
        (antrow_hbm, antrow), (dirs_hbm, dirs), (pointing_hbm, pointing)))]
    for copy in small[:2] + slabs[:1] + small[2:] + slabs[1:]:
        copy.start()
    small[0].wait()
    r, c = lax.axis_index("row"), lax.axis_index("col")
    me = r * COLS + c

    def peer(i):
        k, j = lax.rem(i, COLS), lax.div(i, COLS)
        return lax.rem(r + j + 3 * k, ROWS), lax.rem(c + k, COLS)

    pos[...] = jnp.zeros((1, 128), F32)
    for xy in range(2):
        pos[0:1, xy * LOCAL:(xy + 1) * LOCAL] = place[xy:xy + 1, :]

    barrier = pltpu.get_barrier_semaphore()

    def greet(first, count):
        for v in range(count):
            pl.semaphore_signal(barrier, inc=1, device_id=peer(first + v), device_id_type=MESH)

    def launch(chunk, first, count):
        for v in range(count):
            rt, ct = peer(first + v)
            pltpu.make_async_remote_copy(
                src_ref=send.at[chunk, rt * COLS + ct], dst_ref=recv.at[chunk, me],
                send_sem=ssem.at[chunk], recv_sem=rsem.at[chunk],
                device_id=(rt, ct), device_id_type=MESH).start()

    def own(chunk):
        return pltpu.make_async_copy(send.at[chunk, me], recv.at[chunk, me], lsem.at[chunk])

    def channelize(chunk):
        slabs[chunk].wait()
        if chunk == 0:
            small[1].wait()
        def filt(u, carry):
            first = chunk * SPC + 8 * u
            for j in range(2):
                halves = []
                for lane in (j * 128, j * 128 + HALF):
                    frames = [
                        samples[:, pl.ds(pl.multiple_of((first + f) * FRAME + lane, 128), 128)].astype(F32)
                        for f in range(8 + TAPS - 1)
                    ]
                    tap = [jnp.broadcast_to(taps[t:t + 1, lane:lane + 128], (8, 128)) for t in range(TAPS)]
                    sums = []
                    for s in range(8):
                        acc = tap[0] * frames[s]
                        for t in range(1, TAPS):
                            acc = acc + tap[t] * frames[s + t]
                        sums.append(acc)
                    halves.append(sums)
                for s in range(8):
                    at = pl.ds(8 * u + s, 8, stride=PITCH)
                    eo[j, at, :] = halves[0][s] + halves[1][s]
                    eo[2 + j, at, :] = halves[0][s] - halves[1][s]
            if chunk > 0:
                launch(chunk - 1, 1 + 5 * u, 5)
            return carry

        if chunk == 0:
            def greeting(u, carry):
                greet(1 + 8 * u, 8)
                return filt(u, carry)
            lax.fori_loop(0, SPC // 8 - 1, greeting, 0)
            greet(DEVICES - 7, 7)
            filt(SPC // 8 - 1, 0)
        else:
            lax.fori_loop(0, SPC // 8, filt, 0)

        if chunk == 0:
            for copy in small[2:4]:
                copy.wait()

        def dft(g, carry):
            for p in range(2):
                x = jnp.concatenate([
                    jnp.concatenate([eo[2 * p + j, pl.ds((2 * g + i) * PITCH, SPC), :] for j in range(2)], 1)
                    for i in range(2)], 0)
                hi = x.astype(BF16)
                lo = (x - hi.astype(F32)).astype(BF16)
                res = lax.dot_general(thigh[p], hi, NT, preferred_element_type=F32)
                res = res + lax.dot_general(thigh[p], lo, NT, preferred_element_type=F32)
                res = res + lax.dot_general(tlow[p], hi, NT, preferred_element_type=F32)
                for q in range(2):
                    for i in range(2):
                        stage[pl.ds(p * 16 + q * 8 + i + 2 * g, 128, stride=BLOCK), :] = (
                            res[q * 128:(q + 1) * 128, i * 128:(i + 1) * 128])
            if chunk > 0:
                launch(chunk - 1, 81 + 8 * g, 8)
            return carry
        lax.fori_loop(0, LOCAL // 2, dft, 0)

        def pack(u, carry):
            for d in range(8):
                block = stage[pl.ds((u * 8 + d) * BLOCK, 32), :]
                send[chunk, u * 8 + d] = block.astype(BF16)
            return carry

        def packing(u, carry):
            if chunk > 0:
                launch(chunk - 1, 113 + u, 1)
            return pack(u, carry)
        lax.fori_loop(0, 15, packing, 0)
        pack(15, 0)
        if chunk > 0:
            own(chunk - 1).start()

    channelize(0)
    pl.semaphore_wait(barrier, DEVICES - 1)
    pltpu.make_async_copy(pos, pos1.at[r], lsem.at[3]).start()
    for j in range(1, ROWS):
        pltpu.make_async_remote_copy(
            src_ref=pos, dst_ref=pos1.at[r], send_sem=psem.at[0], recv_sem=psem.at[1],
            device_id=(lax.rem(r + j, ROWS), c), device_id_type=MESH).start()
    channelize(1)
    pltpu.make_async_copy(pos, pos1.at[r], lsem.at[3]).wait()
    pltpu.make_async_copy(pos1.at[pl.ds(0, ROWS - 1)], pos1.at[pl.ds(0, ROWS - 1)], psem.at[0]).wait()
    pltpu.make_async_copy(pos1.at[pl.ds(0, ROWS - 1)], pos1.at[pl.ds(0, ROWS - 1)], psem.at[1]).wait()
    pltpu.make_async_copy(pos1, pos2.at[c], lsem.at[3]).start()
    for k in range(1, COLS):
        pltpu.make_async_remote_copy(
            src_ref=pos1, dst_ref=pos2.at[c], send_sem=qsem.at[0], recv_sem=qsem.at[1],
            device_id=(r, lax.rem(c + k, COLS)), device_id_type=MESH).start()
    channelize(2)
    own(2).start()

    for copy in small[4:]:
        copy.wait()
    lane = lax.broadcasted_iota(jnp.int32, (128, 128), 1).astype(F32)
    for blk in range(8):
        wanted = column(antrow[blk:blk + 1, :])
        for t in range(8):
            perm[blk * 128:(blk + 1) * 128, t * 128:(t + 1) * 128] = (
                jnp.where(wanted == lane + 128.0 * t, 1.0, 0.0).astype(BF16))
        wanted = column(pointing[blk:blk + 1, :])
        l_sum = jnp.zeros((128, 128), F32)
        m_sum = jnp.zeros((128, 128), F32)
        for t in range(8):
            hit = wanted == lane + 128.0 * t
            l_sum = l_sum + jnp.where(hit, dirs[0:1, t * 128:(t + 1) * 128], 0.0)
            m_sum = m_sum + jnp.where(hit, dirs[1:2, t * 128:(t + 1) * 128], 0.0)
        lcol[blk * 128:(blk + 1) * 128, :] = jnp.broadcast_to(jnp.sum(l_sum, 1, keepdims=True), (128, 128))
        mcol[blk * 128:(blk + 1) * 128, :] = jnp.broadcast_to(jnp.sum(m_sum, 1, keepdims=True), (128, 128))

    pltpu.make_async_copy(pos1, pos2.at[c], lsem.at[3]).wait()
    for s in range(2):
        pltpu.make_async_copy(pos2.at[pl.ds(0, COLS - 1)], pos2.at[pl.ds(0, COLS - 1)], qsem.at[s]).wait()

    def spread(i, carry):
        table[pl.ds(i, 1), :] = pos2[i // ROWS, i % ROWS]
        return carry
    lax.fori_loop(0, DEVICES, spread, 0)

    def thirds(rest):
        parts = []
        for _ in range(3):
            part = rest.astype(BF16)
            rest = rest - part.astype(F32)
            parts.append(part)
        return parts
    parts = thirds(table[...])
    picked = []
    antenna = lax.broadcasted_iota(jnp.int32, (128, ANT), 1)
    entry = lax.broadcasted_iota(jnp.int32, (128, ANT), 0)
    mine = (entry % ROWS) * COLS + entry // ROWS == antenna // LOCAL
    for xy in range(2):
        pick = jnp.where(entry == antenna % LOCAL + LOCAL * xy, 1.0, 0.0).astype(BF16)
        whole = sum(lax.dot_general(part, pick, NN, preferred_element_type=F32) for part in parts[::-1])
        picked.append(jnp.sum(jnp.where(mine, whole, 0.0), 0, keepdims=True))
    split = [part.astype(F32) for along in picked for part in thirds(along)]
    split = jnp.concatenate(split + [jnp.zeros((2, ANT), F32)], 0).astype(BF16)
    moved = lax.dot_general(split, perm[...], NN, preferred_element_type=F32)
    xpos = (moved[2:3] + moved[1:2]) + moved[0:1]
    ypos = (moved[5:6] + moved[4:5]) + moved[3:4]

    factors = [(2 * me + p + 1).astype(F32) * (1.0 / CHANNELS) for p in range(2)]

    def weigh(u, carry):
        rows = pl.ds(pl.multiple_of(u * 16, 16), 16)
        l_here, m_here = lcol[rows, :], mcol[rows, :]
        for t in range(8):
            cols = slice(t * 128, (t + 1) * 128)
            delay = l_here * xpos[:, cols] + m_here * ypos[:, cols]
            for p in range(2):
                turns = delay * factors[p]
                turns = turns - jnp.round(turns)
                weights[p, rows, t * 128:(t + 1) * 128] = sine(0.25 - jnp.abs(turns)).astype(BF16)
                w = 0.25 - jnp.abs(0.25 - turns)
                weights[p, rows, ANT + t * 128:ANT + (t + 1) * 128] = sine(jnp.maximum(w, -0.5 - w)).astype(BF16)
        return carry

    def weighing(u, carry):
        launch(CHUNKS - 1, 1 + 2 * u, 2)
        return weigh(u, carry)
    lax.fori_loop(0, BEAMS // 16 - 1, weighing, 0)
    launch(CHUNKS - 1, DEVICES - 1, 1)
    weigh(BEAMS // 16 - 1, 0)

    def beams(chunk, carry):
        own(chunk).wait()
        every = pl.ds(0, DEVICES - 1)
        pltpu.make_async_copy(send.at[chunk, every], recv.at[chunk, every], rsem.at[chunk]).wait()
        lanes = pl.ds(pl.multiple_of(chunk * 256, 256), 256)
        bins_at = pl.ds(pl.multiple_of(chunk * 8, 8), 8)

        def gather(u, carry):
            rows = pl.ds(pl.multiple_of(u * 128, 128), 128)
            below = pl.ds(pl.multiple_of(ANT + u * 128, 128), 128)
            z = recv[chunk, pl.ds(u * 16, 16)].astype(F32)
            for p in range(2):
                re = z[:, p * 16:p * 16 + 8, :].reshape(128, 128)
                im = z[:, p * 16 + 8:p * 16 + 16, :].reshape(128, 128)
                full[p, rows, 0:128] = re.astype(BF16)
                full[p, rows, 128:256] = im.astype(BF16)
                full[p, below, 0:128] = im.astype(BF16)
                full[p, below, 128:256] = (-re).astype(BF16)
            return carry
        lax.fori_loop(0, 8, gather, 0)
        for p in range(2):
            v = lax.dot_general(weights[p], full[p], NN, preferred_element_type=F32)
            power = v[:, 0:128] * v[:, 0:128] + v[:, 128:256] * v[:, 128:256]
            bins = jnp.sum(jnp.transpose(power).reshape(SPC // INTEG, INTEG, BEAMS), axis=1)
            beam[p, bins_at, :] = bins
            x = lax.dot_general(perm[...], full[p, 0:ANT, :], NN, preferred_element_type=F32)
            xs[p, :, lanes] = x.astype(BF16)
        return carry
    lax.fori_loop(0, CHUNKS, beams, 0)

    for chunk in range(CHUNKS):
        every = pl.ds(0, DEVICES - 1)
        pltpu.make_async_copy(send.at[chunk, every], recv.at[chunk, every], ssem.at[chunk]).wait()


def gram_kernel(x, out, kept):
    u = pl.program_id(1)
    scale = 1.0 / SPECTRA

    def panel(b):
        lo, hi = b * 256, (b + 1) * 256
        right = x[0, lo:hi, :]
        turned = jnp.concatenate(
            [piece for k in range(CHUNKS) for piece in (-right[:, k * 256 + 128:(k + 1) * 256], right[:, k * 256:k * 256 + 128])], 1)
        for q, other in enumerate((right, turned)):
            col = lax.dot_general(x[0, lo:, :], other, NT, preferred_element_type=F32) * scale
            out[0, q, :, lo:hi] = col[0:256]
            if hi < ANT:
                kept[q, hi:, lo:hi] = col[256:]
            for j in range(b + 1, ANT // 256):
                flip = jnp.transpose(col[(j - b) * 256:(j - b + 1) * 256])
                out[0, q, :, j * 256:(j + 1) * 256] = -flip if q else flip
            if lo > 0:
                out[0, q, :, 0:lo] = kept[q, lo:hi, 0:lo]

    for b in range(ANT // 256):
        pl.when(u == b)(functools.partial(panel, b))


def body(samples, pfb_taps, antenna_input_row, positions, directions, pointing):
    high, low = dft_tables()
    vmem = pl.BlockSpec(memory_space=pltpu.VMEM)
    xs, beam = pl.pallas_call(
        main_kernel,
        out_shape=(jax.ShapeDtypeStruct((2, ANT, 2 * SPECTRA), BF16),
                   jax.ShapeDtypeStruct((2, SPECTRA // INTEG, BEAMS), F32)),
        in_specs=[pl.BlockSpec(memory_space=pltpu.MemorySpace.HBM)] * 8,
        out_specs=(vmem, vmem),
        scratch_shapes=[
            pltpu.VMEM((4, LOCAL * PITCH, 128), F32),
            pltpu.VMEM((DEVICES * BLOCK, 128), F32),
            pltpu.VMEM((CHUNKS, DEVICES, 32, 128), BF16),
            pltpu.VMEM((CHUNKS, DEVICES, 32, 128), BF16),
            pltpu.VMEM((ROWS, 1, 128), F32),
            pltpu.VMEM((COLS, ROWS, 1, 128), F32),
            pltpu.VMEM((DEVICES, 128), F32),
            pltpu.VMEM((2, BEAMS, 2 * ANT), BF16),
            pltpu.VMEM((ANT, ANT), BF16),
            pltpu.VMEM((BEAMS, 128), F32),
            pltpu.VMEM((BEAMS, 128), F32),
            pltpu.VMEM((2, 2 * ANT, 256), BF16),
            pltpu.VMEM((1, 128), F32),
            pltpu.VMEM((LOCAL, (SPECTRA + TAPS - 1) * FRAME), BF16),
            pltpu.VMEM((TAPS, FRAME), F32),
            pltpu.VMEM((2, HALF, HALF), BF16),
            pltpu.VMEM((2, HALF, HALF), BF16),
            pltpu.VMEM((8, 128), jnp.int32),
            pltpu.VMEM((2, LOCAL), F32),
            pltpu.VMEM((2, ANT), F32),
            pltpu.VMEM((8, 128), jnp.int32),
            pltpu.SemaphoreType.DMA((4,)),
            pltpu.SemaphoreType.DMA((CHUNKS,)),
            pltpu.SemaphoreType.DMA((CHUNKS,)),
            pltpu.SemaphoreType.DMA((2,)),
            pltpu.SemaphoreType.DMA((2,)),
            pltpu.SemaphoreType.DMA((7 + CHUNKS,)),
        ],
        compiler_params=pltpu.CompilerParams(
            collective_id=0, has_side_effects=True, vmem_limit_bytes=63 * 1024 * 1024),
        name="channelize_exchange_beams",
    )(samples, pfb_taps, jnp.asarray(high), jnp.asarray(low), antenna_input_row.reshape(8, 128), positions,
      directions, pointing.reshape(8, 128))
    vis = pl.pallas_call(
        gram_kernel,
        grid=(2, 4),
        out_shape=jax.ShapeDtypeStruct((2, 2, ANT, ANT), F32),
        in_specs=[pl.BlockSpec((1, ANT, 2 * SPECTRA), lambda p, u: (p, 0, 0))],
        out_specs=pl.BlockSpec((1, 2, 256, ANT), lambda p, u: (p, 0, u, 0)),
        scratch_shapes=[pltpu.VMEM((2, ANT, ANT), F32)],
        compiler_params=pltpu.CompilerParams(vmem_limit_bytes=63 * 1024 * 1024),
        name="visibilities",
    )(xs)
    return vis, beam


def solution(mesh):
    return jax.shard_map(
        body,
        mesh=mesh,
        in_specs=(P(("row", "col"), None), P(), P(), P(None, ("row", "col")), P(), P()),
        out_specs=(P(("row", "col"), None, None, None), P(("row", "col"), None, None)),
        check_vma=False,
    )
```

```python
import functools
import math

import jax
import jax.numpy as jnp
import ml_dtypes
import numpy as np
from jax import lax
from jax.experimental import pallas as pl
from jax.experimental.pallas import tpu as pltpu
from jax.sharding import PartitionSpec as P

MESH = pl.DeviceIdType.MESH
ROWS, COLS = 8, 16
DEVICES = ROWS * COLS
ANT = 1024
BEAMS = 1024
LOCAL = 8
FRAME = 512
HALF = 256
TAPS = 8
CHUNKS = 3
SPC = 128
SPECTRA = CHUNKS * SPC
INTEG = 16
PITCH = SPC + 1
BLOCK = 33
CHANNELS = 256
NT = (((1,), (1,)), ((), ()))
NN = (((1,), (0,)), ((), ()))
F32, BF16 = jnp.float32, jnp.bfloat16


def dft_tables():
    n = np.arange(HALF)
    d = np.arange(CHANNELS // 2)
    tables = []
    for parity in range(2):
        angle = 2.0 * np.pi * ((2 * d[:, None] + parity) * n[None, :] % FRAME) / FRAME
        tables.append(np.concatenate([np.cos(angle), -np.sin(angle)], 0) / math.sqrt(FRAME))
    table = np.stack(tables)
    high = table.astype(ml_dtypes.bfloat16)
    low = (table - high.astype(np.float64)).astype(ml_dtypes.bfloat16)
    return high, low


def sine_coefficients():
    theta = (np.arange(4000) + 0.5) * np.pi / 8000
    w = 0.25 * np.cos(theta)
    basis = np.stack([w ** (2 * j + 1) for j in range(5)], 1)
    return np.linalg.lstsq(basis, np.sin(2 * np.pi * w), rcond=None)[0]


SINE = [float(v) / math.sqrt(ANT) for v in sine_coefficients()]


def sine(w):
    z = w * w
    acc = SINE[-1] * z + SINE[-2]
    for coefficient in SINE[-3::-1]:
        acc = acc * z + coefficient
    return acc * w


def column(row):
    return jnp.transpose(jnp.broadcast_to(row.astype(F32), (128, 128)))


def main_kernel(samples_hbm, taps_hbm, thigh_hbm, tlow_hbm, antrow_hbm, place_hbm, dirs_hbm, pointing_hbm,
                xs, beam,
                eo, stage, send, recv, pos1, pos2, table, weights, perm, lcol, mcol, full, pos,
                samples, taps, thigh, tlow, antrow, place, dirs, pointing,
                lsem, ssem, rsem, psem, qsem, isem):
    needed = [0] + [(k * SPC + TAPS - 1) * FRAME for k in range(1, CHUNKS + 1)]
    slabs = [pltpu.make_async_copy(
        samples_hbm.at[:, lo:hi], samples.at[:, lo:hi], isem.at[7 + k])
        for k, (lo, hi) in enumerate(zip(needed[:-1], needed[1:]))]
    small = [pltpu.make_async_copy(src, dst, isem.at[k]) for k, (src, dst) in enumerate((
        (place_hbm, place), (taps_hbm, taps), (thigh_hbm, thigh), (tlow_hbm, tlow),
        (antrow_hbm, antrow), (dirs_hbm, dirs), (pointing_hbm, pointing)))]
    for copy in small[:2] + slabs[:1] + small[2:] + slabs[1:]:
        copy.start()
    small[0].wait()
    r, c = lax.axis_index("row"), lax.axis_index("col")
    me = r * COLS + c

    def peer(i):
        k, j = lax.rem(i, COLS), lax.div(i, COLS)
        return lax.rem(r + j + 3 * k, ROWS), lax.rem(c + k, COLS)

    pos[...] = jnp.zeros((1, 128), F32)
    for xy in range(2):
        pos[0:1, xy * LOCAL:(xy + 1) * LOCAL] = place[xy:xy + 1, :]

    barrier = pltpu.get_barrier_semaphore()

    def greet(first, count):
        for v in range(count):
            pl.semaphore_signal(barrier, inc=1, device_id=peer(first + v), device_id_type=MESH)

    def launch(chunk, first, count):
        for v in range(count):
            rt, ct = peer(first + v)
            pltpu.make_async_remote_copy(
                src_ref=send.at[chunk, rt * COLS + ct], dst_ref=recv.at[chunk, me],
                send_sem=ssem.at[chunk], recv_sem=rsem.at[chunk],
                device_id=(rt, ct), device_id_type=MESH).start()

    def own(chunk):
        return pltpu.make_async_copy(send.at[chunk, me], recv.at[chunk, me], lsem.at[chunk])

    def channelize(chunk):
        slabs[chunk].wait()
        if chunk == 0:
            small[1].wait()
        def filt(u, carry):
            first = chunk * SPC + 8 * u
            for j in range(2):
                halves = []
                for lane in (j * 128, j * 128 + HALF):
                    frames = [
                        samples[:, pl.ds(pl.multiple_of((first + f) * FRAME + lane, 128), 128)].astype(F32)
                        for f in range(8 + TAPS - 1)
                    ]
                    tap = [jnp.broadcast_to(taps[t:t + 1, lane:lane + 128], (8, 128)) for t in range(TAPS)]
                    sums = []
                    for s in range(8):
                        acc = tap[0] * frames[s]
                        for t in range(1, TAPS):
                            acc = acc + tap[t] * frames[s + t]
                        sums.append(acc)
                    halves.append(sums)
                for s in range(8):
                    at = pl.ds(8 * u + s, 8, stride=PITCH)
                    eo[j, at, :] = halves[0][s] + halves[1][s]
                    eo[2 + j, at, :] = halves[0][s] - halves[1][s]
            if chunk > 0:
                launch(chunk - 1, 1 + 5 * u, 5)
            return carry

        if chunk == 0:
            def greeting(u, carry):
                greet(1 + 8 * u, 8)
                return filt(u, carry)
            lax.fori_loop(0, SPC // 8 - 1, greeting, 0)
            greet(DEVICES - 7, 7)
            filt(SPC // 8 - 1, 0)
        else:
            lax.fori_loop(0, SPC // 8, filt, 0)

        if chunk == 0:
            for copy in small[2:4]:
                copy.wait()

        def dft(g, carry):
            for p in range(2):
                x = jnp.concatenate([
                    jnp.concatenate([eo[2 * p + j, pl.ds((2 * g + i) * PITCH, SPC), :] for j in range(2)], 1)
                    for i in range(2)], 0)
                hi = x.astype(BF16)
                lo = (x - hi.astype(F32)).astype(BF16)
                res = lax.dot_general(thigh[p], hi, NT, preferred_element_type=F32)
                res = res + lax.dot_general(thigh[p], lo, NT, preferred_element_type=F32)
                res = res + lax.dot_general(tlow[p], hi, NT, preferred_element_type=F32)
                for q in range(2):
                    for i in range(2):
                        stage[pl.ds(p * 16 + q * 8 + i + 2 * g, 128, stride=BLOCK), :] = (
                            res[q * 128:(q + 1) * 128, i * 128:(i + 1) * 128])
            if chunk > 0:
                launch(chunk - 1, 81 + 8 * g, 8)
            return carry
        lax.fori_loop(0, LOCAL // 2, dft, 0)

        def pack(u, carry):
            for d in range(8):
                block = stage[pl.ds((u * 8 + d) * BLOCK, 32), :]
                send[chunk, u * 8 + d] = block.astype(BF16)
            return carry

        def packing(u, carry):
            if chunk > 0:
                launch(chunk - 1, 113 + u, 1)
            return pack(u, carry)
        lax.fori_loop(0, 15, packing, 0)
        pack(15, 0)
        if chunk > 0:
            own(chunk - 1).start()

    channelize(0)
    pl.semaphore_wait(barrier, DEVICES - 1)
    pltpu.make_async_copy(pos, pos1.at[r], lsem.at[3]).start()
    for j in range(1, ROWS):
        pltpu.make_async_remote_copy(
            src_ref=pos, dst_ref=pos1.at[r], send_sem=psem.at[0], recv_sem=psem.at[1],
            device_id=(lax.rem(r + j, ROWS), c), device_id_type=MESH).start()
    channelize(1)
    pltpu.make_async_copy(pos, pos1.at[r], lsem.at[3]).wait()
    pltpu.make_async_copy(pos1.at[pl.ds(0, ROWS - 1)], pos1.at[pl.ds(0, ROWS - 1)], psem.at[0]).wait()
    pltpu.make_async_copy(pos1.at[pl.ds(0, ROWS - 1)], pos1.at[pl.ds(0, ROWS - 1)], psem.at[1]).wait()
    pltpu.make_async_copy(pos1, pos2.at[c], lsem.at[3]).start()
    for k in range(1, COLS):
        pltpu.make_async_remote_copy(
            src_ref=pos1, dst_ref=pos2.at[c], send_sem=qsem.at[0], recv_sem=qsem.at[1],
            device_id=(r, lax.rem(c + k, COLS)), device_id_type=MESH).start()
    channelize(2)
    own(2).start()

    for copy in small[4:]:
        copy.wait()
    lane = lax.broadcasted_iota(jnp.int32, (128, 128), 1).astype(F32)
    for blk in range(8):
        wanted = column(antrow[blk:blk + 1, :])
        for t in range(8):
            perm[blk * 128:(blk + 1) * 128, t * 128:(t + 1) * 128] = (
                jnp.where(wanted == lane + 128.0 * t, 1.0, 0.0).astype(BF16))
        wanted = column(pointing[blk:blk + 1, :])
        l_sum = jnp.zeros((128, 128), F32)
        m_sum = jnp.zeros((128, 128), F32)
        for t in range(8):
            hit = wanted == lane + 128.0 * t
            l_sum = l_sum + jnp.where(hit, dirs[0:1, t * 128:(t + 1) * 128], 0.0)
            m_sum = m_sum + jnp.where(hit, dirs[1:2, t * 128:(t + 1) * 128], 0.0)
        lcol[blk * 128:(blk + 1) * 128, :] = jnp.broadcast_to(jnp.sum(l_sum, 1, keepdims=True), (128, 128))
        mcol[blk * 128:(blk + 1) * 128, :] = jnp.broadcast_to(jnp.sum(m_sum, 1, keepdims=True), (128, 128))

    pltpu.make_async_copy(pos1, pos2.at[c], lsem.at[3]).wait()
    for s in range(2):
        pltpu.make_async_copy(pos2.at[pl.ds(0, COLS - 1)], pos2.at[pl.ds(0, COLS - 1)], qsem.at[s]).wait()

    def spread(i, carry):
        table[pl.ds(i, 1), :] = pos2[i // ROWS, i % ROWS]
        return carry
    lax.fori_loop(0, DEVICES, spread, 0)

    def thirds(rest):
        parts = []
        for _ in range(3):
            part = rest.astype(BF16)
            rest = rest - part.astype(F32)
            parts.append(part)
        return parts
    parts = thirds(table[...])
    picked = []
    antenna = lax.broadcasted_iota(jnp.int32, (128, ANT), 1)
    entry = lax.broadcasted_iota(jnp.int32, (128, ANT), 0)
    mine = (entry % ROWS) * COLS + entry // ROWS == antenna // LOCAL
    for xy in range(2):
        pick = jnp.where(entry == antenna % LOCAL + LOCAL * xy, 1.0, 0.0).astype(BF16)
        whole = sum(lax.dot_general(part, pick, NN, preferred_element_type=F32) for part in parts[::-1])
        picked.append(jnp.sum(jnp.where(mine, whole, 0.0), 0, keepdims=True))
    split = [part.astype(F32) for along in picked for part in thirds(along)]
    split = jnp.concatenate(split + [jnp.zeros((2, ANT), F32)], 0).astype(BF16)
    moved = lax.dot_general(split, perm[...], NN, preferred_element_type=F32)
    xpos = (moved[2:3] + moved[1:2]) + moved[0:1]
    ypos = (moved[5:6] + moved[4:5]) + moved[3:4]

    factors = [(2 * me + p + 1).astype(F32) * (1.0 / CHANNELS) for p in range(2)]

    def weigh(u, carry):
        rows = pl.ds(pl.multiple_of(u * 16, 16), 16)
        l_here, m_here = lcol[rows, :], mcol[rows, :]
        for t in range(8):
            cols = slice(t * 128, (t + 1) * 128)
            delay = l_here * xpos[:, cols] + m_here * ypos[:, cols]
            for p in range(2):
                turns = delay * factors[p]
                turns = turns - jnp.round(turns)
                weights[p, rows, t * 128:(t + 1) * 128] = sine(0.25 - jnp.abs(turns)).astype(BF16)
                w = 0.25 - jnp.abs(0.25 - turns)
                weights[p, rows, ANT + t * 128:ANT + (t + 1) * 128] = sine(jnp.maximum(w, -0.5 - w)).astype(BF16)
        return carry

    def weighing(u, carry):
        launch(CHUNKS - 1, 1 + 2 * u, 2)
        return weigh(u, carry)
    lax.fori_loop(0, BEAMS // 16 - 1, weighing, 0)
    launch(CHUNKS - 1, DEVICES - 1, 1)
    weigh(BEAMS // 16 - 1, 0)

    def beams(chunk, carry):
        own(chunk).wait()
        every = pl.ds(0, DEVICES - 1)
        pltpu.make_async_copy(send.at[chunk, every], recv.at[chunk, every], rsem.at[chunk]).wait()
        lanes = pl.ds(pl.multiple_of(chunk * 256, 256), 256)
        bins_at = pl.ds(pl.multiple_of(chunk * 8, 8), 8)

        def gather(u, carry):
            rows = pl.ds(pl.multiple_of(u * 128, 128), 128)
            below = pl.ds(pl.multiple_of(ANT + u * 128, 128), 128)
            z = recv[chunk, pl.ds(u * 16, 16)].astype(F32)
            for p in range(2):
                re = z[:, p * 16:p * 16 + 8, :].reshape(128, 128)
                im = z[:, p * 16 + 8:p * 16 + 16, :].reshape(128, 128)
                full[p, rows, 0:128] = re.astype(BF16)
                full[p, rows, 128:256] = im.astype(BF16)
                full[p, below, 0:128] = im.astype(BF16)
                full[p, below, 128:256] = (-re).astype(BF16)
            return carry
        lax.fori_loop(0, 8, gather, 0)
        for p in range(2):
            v = lax.dot_general(weights[p], full[p], NN, preferred_element_type=F32)
            power = v[:, 0:128] * v[:, 0:128] + v[:, 128:256] * v[:, 128:256]
            bins = jnp.sum(jnp.transpose(power).reshape(SPC // INTEG, INTEG, BEAMS), axis=1)
            beam[p, bins_at, :] = bins
            x = lax.dot_general(perm[...], full[p, 0:ANT, :], NN, preferred_element_type=F32)
            xs[p, :, lanes] = x.astype(BF16)
        return carry
    lax.fori_loop(0, CHUNKS, beams, 0)

    for chunk in range(CHUNKS):
        every = pl.ds(0, DEVICES - 1)
        pltpu.make_async_copy(send.at[chunk, every], recv.at[chunk, every], ssem.at[chunk]).wait()


def gram_kernel(x_hbm, out, kept, x, sem):
    p, u = pl.program_id(0), pl.program_id(1)
    fetches = [pltpu.make_async_copy(x_hbm.at[k], x.at[k], sem.at[k]) for k in range(2)]

    @pl.when((p == 0) & (u == 0))
    def _():
        fetches[0].start()
        fetches[1].start()
        fetches[0].wait()

    @pl.when((p == 1) & (u == 0))
    def _():
        fetches[1].wait()

    scale = 1.0 / SPECTRA

    def panel(b):
        lo, hi = b * 256, (b + 1) * 256
        right = x[p, lo:hi, :]
        turned = jnp.concatenate(
            [piece for k in range(CHUNKS) for piece in (-right[:, k * 256 + 128:(k + 1) * 256], right[:, k * 256:k * 256 + 128])], 1)
        for q, other in enumerate((right, turned)):
            col = lax.dot_general(x[p, lo:, :], other, NT, preferred_element_type=F32) * scale
            out[0, q, :, lo:hi] = col[0:256]
            if hi < ANT:
                kept[q, hi:, lo:hi] = col[256:]
            for j in range(b + 1, ANT // 256):
                flip = jnp.transpose(col[(j - b) * 256:(j - b + 1) * 256])
                out[0, q, :, j * 256:(j + 1) * 256] = -flip if q else flip
            if lo > 0:
                out[0, q, :, 0:lo] = kept[q, lo:hi, 0:lo]

    for b in range(ANT // 256):
        pl.when(u == b)(functools.partial(panel, b))


def body(samples, pfb_taps, antenna_input_row, positions, directions, pointing):
    high, low = dft_tables()
    vmem = pl.BlockSpec(memory_space=pltpu.VMEM)
    xs, beam = pl.pallas_call(
        main_kernel,
        out_shape=(jax.ShapeDtypeStruct((2, ANT, 2 * SPECTRA), BF16),
                   jax.ShapeDtypeStruct((2, SPECTRA // INTEG, BEAMS), F32)),
        in_specs=[pl.BlockSpec(memory_space=pltpu.MemorySpace.HBM)] * 8,
        out_specs=(vmem, vmem),
        scratch_shapes=[
            pltpu.VMEM((4, LOCAL * PITCH, 128), F32),
            pltpu.VMEM((DEVICES * BLOCK, 128), F32),
            pltpu.VMEM((CHUNKS, DEVICES, 32, 128), BF16),
            pltpu.VMEM((CHUNKS, DEVICES, 32, 128), BF16),
            pltpu.VMEM((ROWS, 1, 128), F32),
            pltpu.VMEM((COLS, ROWS, 1, 128), F32),
            pltpu.VMEM((DEVICES, 128), F32),
            pltpu.VMEM((2, BEAMS, 2 * ANT), BF16),
            pltpu.VMEM((ANT, ANT), BF16),
            pltpu.VMEM((BEAMS, 128), F32),
            pltpu.VMEM((BEAMS, 128), F32),
            pltpu.VMEM((2, 2 * ANT, 256), BF16),
            pltpu.VMEM((1, 128), F32),
            pltpu.VMEM((LOCAL, (SPECTRA + TAPS - 1) * FRAME), BF16),
            pltpu.VMEM((TAPS, FRAME), F32),
            pltpu.VMEM((2, HALF, HALF), BF16),
            pltpu.VMEM((2, HALF, HALF), BF16),
            pltpu.VMEM((8, 128), jnp.int32),
            pltpu.VMEM((2, LOCAL), F32),
            pltpu.VMEM((2, ANT), F32),
            pltpu.VMEM((8, 128), jnp.int32),
            pltpu.SemaphoreType.DMA((4,)),
            pltpu.SemaphoreType.DMA((CHUNKS,)),
            pltpu.SemaphoreType.DMA((CHUNKS,)),
            pltpu.SemaphoreType.DMA((2,)),
            pltpu.SemaphoreType.DMA((2,)),
            pltpu.SemaphoreType.DMA((7 + CHUNKS,)),
        ],
        compiler_params=pltpu.CompilerParams(
            collective_id=0, has_side_effects=True, vmem_limit_bytes=63 * 1024 * 1024),
        name="channelize_exchange_beams",
    )(samples, pfb_taps, jnp.asarray(high), jnp.asarray(low), antenna_input_row.reshape(8, 128), positions,
      directions, pointing.reshape(8, 128))
    vis = pl.pallas_call(
        gram_kernel,
        grid=(2, 4),
        out_shape=jax.ShapeDtypeStruct((2, 2, ANT, ANT), F32),
        in_specs=[pl.BlockSpec(memory_space=pl.ANY)],
        out_specs=pl.BlockSpec((1, 2, 256, ANT), lambda p, u: (p, 0, u, 0)),
        scratch_shapes=[pltpu.VMEM((2, ANT, ANT), F32), pltpu.VMEM((2, ANT, 2 * SPECTRA), BF16),
                        pltpu.SemaphoreType.DMA((2,))],
        compiler_params=pltpu.CompilerParams(vmem_limit_bytes=63 * 1024 * 1024),
        name="visibilities",
    )(xs)
    return vis, beam


def solution(mesh):
    return jax.shard_map(
        body,
        mesh=mesh,
        in_specs=(P(("row", "col"), None), P(), P(), P(None, ("row", "col")), P(), P()),
        out_specs=(P(("row", "col"), None, None, None), P(("row", "col"), None, None)),
        check_vma=False,
    )
```
